512 devices in a mesh: seq: 64 (over z, x, core), head: 8 (over y).
Axes of the slice: x: 4, y: 8, z: 8, core: 2. Of those that a mesh axis runs over, the one named last changes fastest.
Arguments:
- queries: bfloat16 [65536, 3072], P('seq', 'head'), may hold values from -6 to 6
- keys: bfloat16 [65536, 3072], P('seq', 'head'), may hold values from -6 to 6
- values: bfloat16 [65536, 3072], P('seq', 'head'), may hold values from -6 to 6
- tile_pool: int32 [24, 1024], P('head'), may hold values from 0 to 511, as said below
- tile_lists: int32 [24, 512, 12], P('head', 'seq'), may hold values from 0 to 15, as said below
- key_slot: int32 [512], replicated, may hold values from 0 to 511, as said below
Outputs:
- attended: bfloat16 [65536, 3072], P(('seq', 'head'))
The draws below stay inside these ranges and needn't reach their ends.
Inputs may be any that keep to these rules, and one draw needn't show every extreme that they name: `tile_pool`: for each index i of seq and each group of 3 heads (heads g * 3 onward), the pool entries of those heads for index i (columns i * 16 onward) name tiles whose slots lie on any one index of seq (slot // 8) at most 1 times, and exactly 1 times on some index. `tile_lists`: the 12 entries of one head and one query tile are distinct. `key_slot`: A permutation of the tiles that keeps tiles 0 to 3 at their own slots.
All inputs are finite; a program needn't handle non-finite values.
Results may differ from the reference program's by a relative error of at most 0.0043.
Values may be sent and summed in bfloat16 or wider, within the bound.
A program may use at most 64 MiB of HBM per device.

```python
import jax
import jax.numpy as jnp
from jax import lax

HEADS = 24
HD = 128
TILE = 128
TILES_DEV = 8
LIST = 12
POOL = 16
SHARED = 4
HEADS_DEV = 3
NTILES = 512
POOLS = 1024
TOKENS = 65536
WIDTH = 3072


def slot_table(key):
    others = jax.random.permutation(jax.random.fold_in(key, 21), NTILES - SHARED) + SHARED
    return jnp.concatenate([jnp.arange(SHARED, dtype=jnp.int32), others.astype(jnp.int32)])


def draw_key_slot(key, part):
    return slot_table(key)


def draw_tile_pool(key, part):
    slots_of = slot_table(key)
    inverse = jnp.argsort(slots_of).astype(jnp.int32)
    seq_count = POOLS // POOL
    groups = HEADS // HEADS_DEV
    demand = HEADS_DEV * POOL
    bound_slots = (demand + seq_count - 1) // seq_count

    def one_block(block_key):
        spread = jax.random.permutation(jax.random.fold_in(block_key, 1), bound_slots * seq_count)
        owners = (spread % seq_count)[:demand].astype(jnp.int32)
        local_tiles = jax.random.randint(jax.random.fold_in(block_key, 2), (demand,), 0, TILES_DEV).astype(jnp.int32)
        return inverse[owners * TILES_DEV + local_tiles].reshape(HEADS_DEV, POOL)
    block_keys = jax.random.split(jax.random.fold_in(key, 31), seq_count * groups)
    blocks = jax.vmap(one_block)(block_keys).reshape(seq_count, groups, HEADS_DEV, POOL)
    return blocks.transpose(1, 2, 0, 3).reshape(HEADS, POOLS).astype(jnp.int32)


def draw_tile_lists(key, part):
    row_keys = jax.random.split(jax.random.fold_in(key, 51), HEADS * NTILES)

    def one_row(row_key):
        return jax.random.permutation(row_key, POOL)[:LIST].astype(jnp.int32)
    return jax.vmap(one_row)(row_keys).reshape(HEADS, NTILES, LIST).astype(jnp.int32)


def draw_keys(key, part):
    total_rows = NTILES * TILE
    sample = jax.random.normal(jax.random.fold_in(key, 5), (total_rows, HEADS * HD), jnp.float32)
    return jnp.clip(sample, -6.0, 6.0).astype(jnp.bfloat16)


def draw_queries(key, part):
    total_rows = NTILES * TILE
    sample = jax.random.normal(jax.random.fold_in(key, 7), (total_rows, HEADS * HD), jnp.float32)
    return jnp.clip(sample, -6.0, 6.0).astype(jnp.bfloat16)


def levels(rng, extent, pieces, low, top_value):
    level = 1.0
    for axis_at, shards_of in pieces:
        heights = jax.random.uniform(jax.random.fold_in(jax.random.fold_in(rng, 6), axis_at), (shards_of,), jnp.float32, low / len(pieces), top_value / len(pieces))
        level = level * jnp.repeat(jnp.exp(heights), extent[axis_at] // shards_of).reshape((-1,) + (1,) * (len(extent) - 1 - axis_at))
    return level


def gaussian(stream_key, dims, deviation, reach, cuts=(), kind=jnp.bfloat16):
    values = jax.random.normal(stream_key, dims, jnp.float32) * deviation
    if len(cuts) > 0:
        values = levels(stream_key, dims, cuts, -0.22, 0.18) * values
    return jnp.clip(values, min=-reach, max=reach).astype(kind)


def setup_inputs(seed: int = 0) -> dict:
    key_list = jax.random.split(jax.random.key(seed), 7)
    queries = draw_queries(jax.random.fold_in(key_list[6], 71), 0)
    keys = draw_keys(jax.random.fold_in(key_list[6], 71), 0)
    values = gaussian(key_list[2], (TOKENS, WIDTH), 1.0, 6.0, ((0, 64), (1, 8)))
    tile_pool = draw_tile_pool(jax.random.fold_in(key_list[6], 71), 0)
    tile_lists = draw_tile_lists(jax.random.fold_in(key_list[6], 71), 0)
    key_slot = draw_key_slot(jax.random.fold_in(key_list[6], 71), 0)
    return dict(queries=queries, keys=keys, values=values, tile_pool=tile_pool, tile_lists=tile_lists, key_slot=key_slot)


def reference(queries, keys, values, tile_pool, tile_lists, key_slot):
    scaling = HD ** -0.5
    query_tiles = queries.reshape(NTILES, TILE, HEADS, HD).transpose(2, 0, 1, 3)
    key_tiles = keys.reshape(NTILES, TILE, HEADS, HD).transpose(2, 0, 1, 3)
    value_tiles = values.reshape(NTILES, TILE, HEADS, HD).transpose(2, 0, 1, 3)
    shared_ids = jnp.arange(SHARED).astype(jnp.int32)
    tile_ids = jnp.arange(NTILES).astype(jnp.int32)

    def one_head(member):
        query_head, key_head, value_head, pool_head, lists_head = member

        def one_tile(query_tile, list_row, tile_id):
            entries = ((tile_id // TILES_DEV) * POOL + list_row).astype(jnp.int32)
            chosen = jnp.concatenate([shared_ids, pool_head[entries].astype(jnp.int32)])
            storage = key_slot[chosen].astype(jnp.int32)
            key_sel = key_head[storage].astype(jnp.float32)
            value_sel = value_head[storage].astype(jnp.float32)
            scores = jnp.einsum("qd,jkd->jqk", query_tile.astype(jnp.float32), key_sel) * scaling
            tile_top = jnp.max(scores, -1)
            weights = jnp.exp(scores - tile_top[..., None])
            row_total = jnp.sum(weights, -1)
            rounded = lax.optimization_barrier(weights.astype(jnp.bfloat16)).astype(jnp.float32)
            numerator = jnp.einsum("jqk,jkd->jqd", rounded, value_sel)
            overall = jnp.max(tile_top, 0)
            factor = jnp.exp(tile_top - overall[None, :])
            upper = jnp.sum(factor[..., None] * numerator, 0)
            lower = jnp.sum(factor * row_total, 0)
            return (upper / lower[:, None]).astype(jnp.bfloat16)

        return jax.vmap(one_tile)(query_head, lists_head, tile_ids)

    result = lax.map(one_head, (query_tiles, key_tiles, value_tiles, tile_pool, tile_lists))
    return result.transpose(1, 2, 0, 3).reshape(NTILES * TILE, HEADS * HD)
```

```python
import functools
import math

import jax
import jax.numpy as jnp
from jax import lax
from jax.experimental import pallas as pl
from jax.experimental.pallas import tpu as pltpu
from jax.sharding import PartitionSpec as P

TILE = 128
HD = 128
HEADS = 3
TILES = 8
POOL = 16
SHARED = 4
KEYS = SHARED + POOL
SEQ = 64
PLANE = 8
ZS = 8
YS = 8
QB = 256
SPLITS = ((0, 96), (96, 32))
WINDOW = 12
MESH = pl.DeviceIdType.MESH
SCALE = HD**-0.5 * math.log2(math.e)
BIG = 1e30


def relatives():
    order = []
    for dx in (0, 1, 3, 2):
        for dc in range(2):
            for dz in (4, 3, 5, 2, 6, 1, 7, 0):
                if (dz, dx, dc) != (0, 0, 0):
                    order.append((dz, dx, dc))
    return order


def to_seq(place, copy_args):
    src, dst, send, recv = copy_args
    return pltpu.make_async_remote_copy(
        src, dst, send, recv, device_id={"seq": place}, device_id_type=MESH
    )


def kernel(
    code, holder, q_ref, k_ref, v_ref, bias_ref, out_ref,
    send_k, send_v0, send_v1, recv_k, recv_v0, recv_v1, shared, k_t, v_t,
    k_cat, v_cat, probs, scores, norm, y_send0, y_send1, y_recv0, y_recv1,
    k_send_sem, k_recv_sem, v_send_sem, v_recv_sem, r_send_sem, r_recv_sem,
    p_send_sem, p_recv_sem, y_send_sem, y_recv_sem,
):
    me = lax.axis_index("seq")
    my_y = lax.axis_index("head")
    z, piece = me // PLANE, me % PLANE
    x, core = piece // 2, piece % 2
    dist = jnp.minimum(z, ZS - z)

    barrier = pltpu.get_barrier_semaphore()

    @pl.loop(1, SEQ)
    def _(d):
        pl.semaphore_signal(
            barrier, inc=1, device_id={"seq": (me + d) % SEQ}, device_id_type=MESH
        )

    @pl.loop(1, YS)
    def _(d):
        pl.semaphore_signal(
            barrier, inc=1, device_id={"head": (my_y + d) % YS}, device_id_type=MESH
        )

    for h in range(HEADS):
        for s in range(TILES):
            k_t[h * TILES + s] = k_ref[s * TILE : (s + 1) * TILE, h * HD : (h + 1) * HD]

    @pl.loop(0, SEQ)
    def _(r):
        send_k[r] = k_t[code[r]]

    for h in range(HEADS):
        for s in range(TILES):
            v_t[h * TILES + s] = v_ref[s * TILE : (s + 1) * TILE, h * HD : (h + 1) * HD].T

    @pl.when(me == 0)
    def _():
        for j in range(SHARED):
            for h in range(HEADS):
                rows = slice(h * TILE, (h + 1) * TILE)
                shared[2 * j, rows] = k_ref[j * TILE : (j + 1) * TILE, h * HD : (h + 1) * HD]
                shared[2 * j + 1, rows] = v_t[h * TILES + j]

    recv_k[me] = send_k[me]

    pl.semaphore_wait(barrier, SEQ - 1 + YS - 1)

    def from_root(p):
        return to_seq(p, (shared.at[p], shared.at[p], p_send_sem.at[p], r_recv_sem))

    @pl.when(me == 0)
    def _():
        for p in range(1, PLANE):
            from_root(p).start()

    def along(step, slot):
        place = ((z + step) % ZS) * PLANE + piece
        return to_seq(
            place, (shared.at[piece], shared.at[piece], r_send_sem.at[slot], r_recv_sem)
        )

    def in_plane(q):
        return to_seq(
            z * PLANE + q,
            (shared.at[piece], shared.at[piece], p_send_sem.at[PLANE + q], p_recv_sem.at[piece]),
        )

    up = jnp.logical_and(z < 4, True)
    down = jnp.logical_or(z == 0, z > 5)

    def relay():
        @pl.when(me != 0)
        def _():
            along(1, 0).wait_recv()

        @pl.when(up)
        def _():
            along(1, 0).start()

        @pl.when(down)
        def _():
            along(ZS - 1, 1).start()

        @pl.loop(0, PLANE)
        def _(q):
            @pl.when(jnp.logical_and(q != piece, z * PLANE + q != 0))
            def _():
                in_plane(q).start()

    order = relatives()

    def place_of(rel):
        dz, dx, dc = rel
        return ((z + dz) % ZS) * PLANE + ((x + dx) % 4) * 2 + (core + dc) % 2

    def k_copy(rel, n):
        place = place_of(rel)
        return to_seq(
            place,
            (send_k.at[place], recv_k.at[me], k_send_sem.at[n % WINDOW], k_recv_sem.at[me]),
        )

    for n, rel in enumerate(order):
        if n >= WINDOW:
            k_copy(rel, n).wait_send()
        if n in (4, 16, 26, 36, 46):
            stage = (4, 16, 26, 36, 46).index(n)

            @pl.when(dist == stage)
            def _():
                relay()

        k_copy(rel, n).start()
        if n == 0:
            @pl.loop(0, SEQ)
            def _(r):
                tile = v_t[code[r]]
                send_v0[r] = tile[:96]
                send_v1[r] = tile[96:]

            recv_v0[me] = send_v0[me]
            recv_v1[me] = send_v1[me]

    def v_copy(part, place):
        src, dst = ((send_v0, recv_v0), (send_v1, recv_v1))[part]
        return to_seq(
            place,
            (src.at[place], dst.at[me], v_send_sem.at[part], v_recv_sem.at[part, me]),
        )

    for part in range(2):
        for rel in order:
            v_copy(part, place_of(rel)).start()

    @pl.when(me != 0)
    def _():
        @pl.loop(0, PLANE)
        def _(q):
            @pl.when(q != piece)
            def _():
                to_seq(
                    0, (shared.at[q], shared.at[q], p_send_sem.at[0], p_recv_sem.at[q])
                ).wait_recv()

    @pl.loop(0, SEQ)
    def _(r):
        @pl.when(r != me)
        def _():
            to_seq(
                0, (send_k.at[0], recv_k.at[r], k_send_sem.at[0], k_recv_sem.at[r])
            ).wait_recv()

    @pl.loop(0, HEADS)
    def _(h):
        for j in range(SHARED):
            k_cat[j * TILE : (j + 1) * TILE] = shared[
                2 * j, pl.ds(pl.multiple_of(h * TILE, TILE), TILE)
            ]
        for p in range(POOL):
            lo = (SHARED + p) * TILE
            k_cat[lo : lo + TILE] = recv_k[holder[h * POOL + p]]

        @pl.loop(0, TILES * TILE // QB)
        def _(b):
            q_at = pl.multiple_of(b * QB, QB)
            q_blk = q_ref[pl.ds(q_at, QB), pl.ds(pl.multiple_of(h * HD, HD), HD)]
            scores[...] = lax.dot_general(
                k_cat[...], q_blk, (((1,), (1,)), ((), ())), preferred_element_type=jnp.float32
            )
            bias = bias_ref[h, :, pl.ds(q_at, QB)]
            top = jnp.full((1, QB), -BIG, jnp.float32)
            for j in range(KEYS):
                tile_top = jnp.max(scores[j * TILE : (j + 1) * TILE], 0, keepdims=True)
                top = jnp.maximum(top, tile_top * SCALE - bias[j : j + 1])
            total = jnp.zeros((1, QB), jnp.float32)
            for j in range(KEYS):
                rows = slice(j * TILE, (j + 1) * TILE)
                weights = jnp.exp2(scores[rows] * SCALE - (top + bias[j : j + 1]))
                total = total + jnp.sum(weights, 0, keepdims=True)
                probs[h, rows, pl.ds(q_at, QB)] = weights.astype(jnp.bfloat16)
            norm[h, :, pl.ds(q_at, QB)] = 1.0 / total

    for part in range(2):
        src, recv = ((send_v0, recv_v0), (send_v1, recv_v1))[part]
        y_send, y_recv = ((y_send0, y_recv0), (y_send1, y_recv1))[part]
        d_at, d_size = SPLITS[part]

        @pl.loop(0, SEQ)
        def _(r):
            @pl.when(r != me)
            def _():
                to_seq(
                    0, (src.at[0], recv.at[r], v_send_sem.at[0], v_recv_sem.at[part, r])
                ).wait_recv()

        @pl.loop(0, HEADS)
        def _(h):
            for j in range(SHARED):
                v_cat[h, :d_size, j * TILE : (j + 1) * TILE] = shared[
                    2 * j + 1, pl.ds(pl.multiple_of(h * HD + d_at, 32), d_size)
                ]
            for p in range(POOL):
                lo = (SHARED + p) * TILE
                v_cat[h, :d_size, lo : lo + TILE] = recv[holder[h * POOL + p]]

        def y_copy(t):
            return pltpu.make_async_remote_copy(
                y_send.at[t],
                y_recv.at[my_y],
                y_send_sem.at[part],
                y_recv_sem.at[part, my_y],
                device_id={"head": t},
                device_id_type=MESH,
            )

        def send_pair(b):
            for i in range(QB // TILE):
                t = b * (QB // TILE) + i

                @pl.when(t != my_y)
                def _():
                    y_copy(t).start()

        blocks = TILES * TILE // QB

        def block_of(i):
            return (my_y // 2 + (2, 1, 3, 0)[i]) % blocks

        for i in range(blocks):
            b = block_of(i)
            q_at = pl.multiple_of(b * QB, QB)

            @pl.loop(0, HEADS)
            def _(h):
                o = jnp.dot(
                    v_cat[h, :d_size], probs[h, :, pl.ds(q_at, QB)],
                    preferred_element_type=jnp.float32,
                )
                o = (o * norm[h, :, pl.ds(q_at, QB)]).astype(jnp.bfloat16)
                for k in range(QB // TILE):
                    y_send[
                        b * (QB // TILE) + k, pl.ds(pl.multiple_of(h * d_size, 32), d_size)
                    ] = o[:, k * TILE : (k + 1) * TILE]

            if i > 0:
                send_pair(block_of(i - 1))
        y_recv[my_y] = y_send[my_y]
        send_pair(block_of(blocks - 1))

    for part in range(2):
        y_send, y_recv = ((y_send0, y_recv0), (y_send1, y_recv1))[part]

        @pl.loop(0, YS)
        def _(g):
            @pl.when(g != my_y)
            def _():
                pltpu.make_async_remote_copy(
                    y_send.at[0], y_recv.at[g], y_send_sem.at[part], y_recv_sem.at[part, g],
                    device_id={"head": 0}, device_id_type=MESH,
                ).wait_recv()

    for g in range(YS):
        for h in range(HEADS):
            both = jnp.concatenate(
                [y_recv0[g, h * 96 : (h + 1) * 96], y_recv1[g, h * 32 : (h + 1) * 32]], 0
            )
            lo = (g * HEADS + h) * HD
            out_ref[:, lo : lo + HD] = both.T

    for n in range(WINDOW):
        k_copy(order[0], n).wait_send()
    for part in range(2):
        @pl.loop(0, SEQ - 1)
        def _(r):
            v_copy(part, 0).wait_send()

        y_send, y_recv = ((y_send0, y_recv0), (y_send1, y_recv1))[part]

        @pl.loop(0, YS - 1)
        def _(r):
            pltpu.make_async_remote_copy(
                y_send.at[0], y_recv.at[0], y_send_sem.at[part], y_recv_sem.at[part, 0],
                device_id={"head": 0}, device_id_type=MESH,
            ).wait_send()

    @pl.when(me == 0)
    def _():
        for p in range(1, PLANE):
            from_root(p).wait_send()

    @pl.when(up)
    def _():
        along(1, 0).wait_send()

    @pl.when(down)
    def _():
        along(ZS - 1, 1).wait_send()

    @pl.loop(0, PLANE)
    def _(q):
        @pl.when(jnp.logical_and(q != piece, z * PLANE + q != 0))
        def _():
            in_plane(q).wait_send()


def body(queries, keys, values, tile_pool, tile_lists, key_slot):
    me = lax.axis_index("seq")
    slots = me * TILES + jnp.arange(TILES, dtype=jnp.int32)
    ids = jnp.arange(key_slot.shape[0], dtype=jnp.int32)
    stored = jnp.sum(jnp.where(key_slot[None] == slots[:, None], ids[None], 0), 1)
    wanted = (tile_pool.reshape(HEADS, SEQ, POOL)[..., None] == stored).astype(jnp.int32)
    codes = jnp.arange(HEADS * TILES, dtype=jnp.int32).reshape(HEADS, 1, 1, TILES)
    code = jnp.sum(wanted * codes, (0, 2, 3))
    own = lax.dynamic_slice_in_dim(tile_pool, me * POOL, POOL, 1).reshape(-1)
    holder = jnp.sum(jnp.where(own[:, None] == ids[None], key_slot[None] // TILES, 0), 1)
    listed = jnp.any(
        tile_lists[:, None] == jnp.arange(POOL, dtype=jnp.int32)[None, :, None, None], -1
    )
    bias = jnp.where(listed, 0.0, BIG).astype(jnp.float32)
    bias = jnp.concatenate([jnp.zeros((HEADS, SHARED, TILES), jnp.float32), bias], 1)
    bias = jnp.repeat(bias, TILE, 2)

    smem = pl.BlockSpec(memory_space=pltpu.SMEM)
    vmem = pl.BlockSpec(memory_space=pltpu.VMEM)
    bf16, f32 = jnp.bfloat16, jnp.float32
    dma = pltpu.SemaphoreType.DMA
    d0, d1 = SPLITS[0][1], SPLITS[1][1]
    return pl.pallas_call(
        kernel,
        out_shape=jax.ShapeDtypeStruct((TILE, YS * HEADS * HD), bf16),
        in_specs=[smem] * 2 + [vmem] * 4,
        out_specs=vmem,
        scratch_shapes=[
            pltpu.VMEM((SEQ, TILE, HD), bf16),
            pltpu.VMEM((SEQ, d0, TILE), bf16),
            pltpu.VMEM((SEQ, d1, TILE), bf16),
            pltpu.VMEM((SEQ, TILE, HD), bf16),
            pltpu.VMEM((SEQ, d0, TILE), bf16),
            pltpu.VMEM((SEQ, d1, TILE), bf16),
            pltpu.VMEM((PLANE, HEADS * TILE, TILE), bf16),
            pltpu.VMEM((HEADS * TILES, TILE, HD), bf16),
            pltpu.VMEM((HEADS * TILES, HD, TILE), bf16),
            pltpu.VMEM((KEYS * TILE, HD), bf16),
            pltpu.VMEM((HEADS, d0, KEYS * TILE), bf16),
            pltpu.VMEM((HEADS, KEYS * TILE, TILES * TILE), bf16),
            pltpu.VMEM((KEYS * TILE, QB), f32),
            pltpu.VMEM((HEADS, 1, TILES * TILE), f32),
            pltpu.VMEM((TILES, HEADS * d0, TILE), bf16),
            pltpu.VMEM((TILES, HEADS * d1, TILE), bf16),
            pltpu.VMEM((YS, HEADS * d0, TILE), bf16),
            pltpu.VMEM((YS, HEADS * d1, TILE), bf16),
            dma((WINDOW,)),
            dma((SEQ,)),
            dma((2,)),
            dma((2, SEQ)),
            dma((2,)),
            dma,
            dma((2 * PLANE,)),
            dma((PLANE,)),
            dma((2,)),
            dma((2, YS)),
        ],
        compiler_params=pltpu.CompilerParams(
            collective_id=0, has_side_effects=True, vmem_limit_bytes=60 * 2**20
        ),
        name="attend",
    )(code, holder, queries, keys, values, bias)


def solution(mesh):
    return jax.shard_map(
        body,
        mesh=mesh,
        in_specs=(
            P("seq", "head"),
            P("seq", "head"),
            P("seq", "head"),
            P("head", None),
            P("head", "seq", None),
            P(),
        ),
        out_specs=P(("seq", "head"), None),
        check_vma=False,
    )
```

```python
import functools
import math

import jax
import jax.numpy as jnp
from jax import lax
from jax.experimental import pallas as pl
from jax.experimental.pallas import tpu as pltpu
from jax.sharding import PartitionSpec as P

TILE = 128
HD = 128
HEADS = 3
TILES = 8
POOL = 16
LIST = 12
SHARED = 4
KEYS = SHARED + POOL
SEQ = 64
PLANE = 8
ZS = 8
YS = 8
QB = 256
SPLITS = ((0, 64), (64, 32), (96, 32))
PARTS = len(SPLITS)
WINDOW = 12
STAGES = (24, 40, 56, 75, 97)
MESH = pl.DeviceIdType.MESH
SCALE = HD**-0.5 * math.log2(math.e)
BIG = 1e30


def relatives():
    order = []
    for dx in (0, 1, 3, 2):
        for dc in range(2):
            for dz in (4, 3, 5, 2, 6, 1, 7, 0):
                if (dz, dx, dc) != (0, 0, 0):
                    order.append((dz, dx, dc))
    return order


def to_seq(place, copy_args):
    src, dst, send, recv = copy_args
    return pltpu.make_async_remote_copy(
        src, dst, send, recv, device_id={"seq": place}, device_id_type=MESH
    )


def kernel(
    q_hbm, k_hbm, v_hbm, pool_hbm, lists_hbm, slot_hbm, *refs,
):
    y_recv, refs = refs[:PARTS], refs[PARTS:]
    v_send, refs = refs[:PARTS], refs[PARTS:]
    v_recv, refs = refs[:PARTS], refs[PARTS:]
    y_send, refs = refs[:PARTS], refs[PARTS:]
    (
        q_ref, k_ref, v_ref, pool_ref, lists_ref, slot_ref, pool_s, slot_s, table_v, table,
        k_send, k_recv, shared, k_t, v_t, bias_ref, k_cat, v_cat, probs, scores, norm,
        load_sem, table_sem, w_send_sem, k_recv_sem, v_send_sem, v_recv_sem,
        r_send_sem, r_recv_sem, p_send_sem, p_recv_sem, y_send_sem, y_recv_sem,
    ) = refs
    me = lax.axis_index("seq")
    my_y = lax.axis_index("head")
    z, piece = me // PLANE, me % PLANE
    x, core = piece // 2, piece % 2
    dist = jnp.minimum(z, ZS - z)

    loads = [
        pltpu.make_async_copy(src, dst, load_sem.at[n])
        for n, (src, dst) in enumerate(
            (
                (slot_hbm, slot_ref),
                (pool_hbm, pool_ref),
                (k_hbm, k_ref),
                (v_hbm, v_ref),
                (lists_hbm, lists_ref),
                (q_hbm, q_ref),
                (pool_hbm, pool_s),
                (slot_hbm, slot_s),
            )
        )
    ]
    for load in loads:
        load.start()

    barrier = pltpu.get_barrier_semaphore()

    @pl.loop(1, SEQ)
    def _(d):
        pl.semaphore_signal(
            barrier, inc=1, device_id={"seq": (me + d) % SEQ}, device_id_type=MESH
        )

    @pl.loop(1, YS)
    def _(d):
        pl.semaphore_signal(
            barrier, inc=1, device_id={"head": (my_y + d) % YS}, device_id_type=MESH
        )

    loads[0].wait()
    loads[1].wait()
    f32, bf16, i32 = jnp.float32, jnp.bfloat16, jnp.int32
    ntiles, entries = slot_ref.shape[1], SEQ * POOL
    mine = me * TILES + lax.broadcasted_iota(i32, (TILES, ntiles), 0)
    ids = lax.broadcasted_iota(i32, (TILES, ntiles), 1)
    stored = jnp.sum(jnp.where(slot_ref[...] == mine, ids, 0), 1, keepdims=True)
    wanted = jnp.zeros((TILES, entries), i32)
    local = lax.broadcasted_iota(i32, (TILES, entries), 0)
    for h in range(HEADS):
        wanted = wanted + jnp.where(pool_ref[h : h + 1, :] == stored, local + h * TILES, 0)
    wanted = jnp.sum(wanted, 0, keepdims=True)
    for shift in (1, 2, 4, 8):
        wanted = wanted + pltpu.roll(wanted, shift, 1)
    table_v[...] = jnp.clip(wanted, 0, HEADS * TILES - 1)
    to_table = pltpu.make_async_copy(table_v, table, table_sem)
    to_table.start()

    def code(r):
        return jnp.clip(table[0, r * POOL + POOL - 1], 0, HEADS * TILES - 1)

    def holder(h, p):
        tile = jnp.clip(pool_s[h, me * POOL + p], 0, ntiles - 1)
        return jnp.clip(slot_s[0, tile] // TILES, 0, SEQ - 1)

    loads[2].wait()
    for h in range(HEADS):
        for s in range(TILES):
            k_t[h * TILES + s] = k_ref[s * TILE : (s + 1) * TILE, h * HD : (h + 1) * HD]
    to_table.wait()

    @pl.loop(0, SEQ)
    def _(r):
        k_send[r] = k_t[code(r)]

    @pl.when(me == 0)
    def _():
        for j in range(SHARED):
            for h in range(HEADS):
                shared[2 * j, h * TILE : (h + 1) * TILE] = k_t[h * TILES + j]

    k_recv[me] = k_send[me]

    pl.semaphore_wait(barrier, SEQ - 1 + YS - 1)

    def from_root(p):
        return to_seq(p, (shared.at[p], shared.at[p], p_send_sem.at[p], r_recv_sem))

    @pl.when(me == 0)
    def _():
        for p in range(2, PLANE, 2):
            from_root(p).start()

    def along(step, slot):
        place = ((z + step) % ZS) * PLANE + piece
        return to_seq(
            place, (shared.at[piece], shared.at[piece], r_send_sem.at[slot], r_recv_sem)
        )

    def in_plane(q):
        return to_seq(
            z * PLANE + q,
            (shared.at[piece], shared.at[piece], p_send_sem.at[PLANE + q], p_recv_sem.at[piece]),
        )

    up = z < 4
    down = jnp.logical_or(z == 0, z > 5)

    def relay():
        @pl.when(me != 0)
        def _():
            along(1, 0).wait_recv()

        @pl.when(up)
        def _():
            along(1, 0).start()

        @pl.when(down)
        def _():
            along(ZS - 1, 1).start()

        @pl.loop(0, PLANE)
        def _(q):
            @pl.when(jnp.logical_and(q != piece, z * PLANE + q != 0))
            def _():
                in_plane(q).start()

    def pack_values():
        loads[3].wait()
        for h in range(HEADS):
            for s in range(TILES):
                v_t[h * TILES + s] = flip(
                    v_ref[s * TILE : (s + 1) * TILE, h * HD : (h + 1) * HD]
                )

        @pl.when(me == 0)
        def _():
            for j in range(SHARED):
                for h in range(HEADS):
                    shared[2 * j + 1, h * TILE : (h + 1) * TILE] = v_t[h * TILES + j]

        @pl.loop(0, SEQ)
        def _(r):
            tile = v_t[code(r)]
            for (d_at, d_size), send in zip(SPLITS, v_send):
                send[r] = tile[d_at : d_at + d_size]

        for send, recv in zip(v_send, v_recv):
            recv[me] = send[me]

        @pl.when(me == 0)
        def _():
            for p in range(1, PLANE, 2):
                from_root(p).start()

    def make_bias():
        loads[4].wait()
        pool_ids = lax.broadcasted_iota(i32, (TILES, POOL), 1)
        spread = (
            lax.broadcasted_iota(i32, (TILES, TILES * TILE), 1) // TILE
            == lax.broadcasted_iota(i32, (TILES, TILES * TILE), 0)
        ).astype(bf16)
        for h in range(HEADS):
            listed = jnp.zeros((TILES, POOL), f32)
            for l in range(LIST):
                listed = jnp.where(lists_ref[h, :, l : l + 1] == pool_ids, 1.0, listed)
            rows = lax.dot_general(
                listed.astype(bf16), spread, (((0,), (0,)), ((), ())), preferred_element_type=f32
            )
            bias_ref[h] = jnp.where(rows > 0.5, 0.0, BIG)

    order = relatives()

    def place_of(rel):
        dz, dx, dc = rel
        return ((z + dz) % ZS) * PLANE + ((x + dx) % 4) * 2 + (core + dc) % 2

    def k_copy(rel, n):
        place = place_of(rel)
        sem = w_send_sem.at[n % WINDOW]
        return to_seq(place, (k_send.at[place], k_recv.at[me], sem, k_recv_sem.at[me]))

    def v_copy(part, place, sem):
        return to_seq(
            place,
            (v_send[part].at[place], v_recv[part].at[me], sem, v_recv_sem.at[part, me]),
        )

    def windowed(n):
        if n < SEQ - 1:
            return k_copy(order[n], n)
        rel = order[n - SEQ + 1]
        return v_copy(0, place_of(rel), w_send_sem.at[n % WINDOW])

    count = STAGES[-1] + 1
    for n in range(count):
        if n == WINDOW:
            pack_values()
            make_bias()
        if n >= WINDOW:
            windowed(n - WINDOW).wait_send()
        if n in STAGES:

            @pl.when(dist == STAGES.index(n))
            def _():
                relay()

        windowed(n).start()
    for n in range(count, 2 * (SEQ - 1)):
        v_copy(0, place_of(order[n - SEQ + 1]), v_send_sem.at[0]).start()
    for part in range(1, PARTS):
        for rel in order:
            v_copy(part, place_of(rel), v_send_sem.at[part]).start()

    @pl.when(me != 0)
    def _():
        @pl.loop(0, PLANE)
        def _(q):
            @pl.when(q != piece)
            def _():
                to_seq(
                    0, (shared.at[q], shared.at[q], p_send_sem.at[0], p_recv_sem.at[q])
                ).wait_recv()

    loads[6].wait()
    loads[7].wait()

    @pl.loop(0, SEQ)
    def _(r):
        @pl.when(r != me)
        def _():
            to_seq(
                0, (k_send.at[0], k_recv.at[r], w_send_sem.at[0], k_recv_sem.at[r])
            ).wait_recv()

    loads[5].wait()

    @pl.loop(0, HEADS)
    def _(h):
        for j in range(SHARED):
            k_cat[j * TILE : (j + 1) * TILE] = shared[
                2 * j, pl.ds(pl.multiple_of(h * TILE, TILE), TILE)
            ]
        for p in range(POOL):
            lo = (SHARED + p) * TILE
            k_cat[lo : lo + TILE] = k_recv[holder(h, p)]

        @pl.loop(0, TILES * TILE // QB)
        def _(b):
            q_at = pl.multiple_of(b * QB, QB)
            q_blk = q_ref[pl.ds(q_at, QB), pl.ds(pl.multiple_of(h * HD, HD), HD)]
            scores[...] = lax.dot_general(
                k_cat[...], q_blk, (((1,), (1,)), ((), ())), preferred_element_type=f32
            )
            bias = bias_ref[h, :, pl.ds(q_at, QB)]
            top = jnp.full((1, QB), -BIG, f32)
            for j in range(KEYS):
                tile_top = jnp.max(scores[j * TILE : (j + 1) * TILE], 0, keepdims=True) * SCALE
                if j >= SHARED:
                    tile_top = tile_top - bias[j - SHARED : j - SHARED + 1]
                top = jnp.maximum(top, tile_top)
            total = jnp.zeros((1, QB), f32)
            for j in range(KEYS):
                rows = slice(j * TILE, (j + 1) * TILE)
                less = top
                if j >= SHARED:
                    less = top + bias[j - SHARED : j - SHARED + 1]
                weights = jnp.exp2(scores[rows] * SCALE - less)
                total = total + jnp.sum(weights, 0, keepdims=True)
                probs[h, rows, pl.ds(q_at, QB)] = weights.astype(bf16)
            norm[h, :, pl.ds(q_at, QB)] = 1.0 / total

    for part in range(PARTS):
        d_at, d_size = SPLITS[part]

        @pl.loop(0, SEQ)
        def _(r):
            @pl.when(r != me)
            def _():
                to_seq(
                    0,
                    (
                        v_send[part].at[0],
                        v_recv[part].at[r],
                        v_send_sem.at[0],
                        v_recv_sem.at[part, r],
                    ),
                ).wait_recv()

        @pl.loop(0, HEADS)
        def _(h):
            for j in range(SHARED):
                v_cat[h, :d_size, j * TILE : (j + 1) * TILE] = shared[
                    2 * j + 1, pl.ds(pl.multiple_of(h * HD + d_at, 32), d_size)
                ]
            for p in range(POOL):
                lo = (SHARED + p) * TILE
                v_cat[h, :d_size, lo : lo + TILE] = v_recv[part][holder(h, p)]

        def y_copy(t):
            return pltpu.make_async_remote_copy(
                y_send[part].at[t],
                y_recv[part].at[my_y],
                y_send_sem.at[part],
                y_recv_sem.at[part, my_y],
                device_id={"head": t},
                device_id_type=MESH,
            )

        def send_pair(b):
            for i in range(QB // TILE):
                t = b * (QB // TILE) + i

                @pl.when(t != my_y)
                def _():
                    y_copy(t).start()

        blocks = TILES * TILE // QB

        def block_of(i):
            return (my_y // 2 + (2, 1, 3, 0)[i]) % blocks

        for i in range(blocks):
            b = block_of(i)
            q_at = pl.multiple_of(b * QB, QB)

            @pl.loop(0, HEADS)
            def _(h):
                o = jnp.dot(
                    v_cat[h, :d_size], probs[h, :, pl.ds(q_at, QB)], preferred_element_type=f32
                )
                o = (o * norm[h, :, pl.ds(q_at, QB)]).astype(bf16)
                for k in range(QB // TILE):
                    y_send[part][
                        b * (QB // TILE) + k, pl.ds(pl.multiple_of(h * d_size, 32), d_size)
                    ] = o[:, k * TILE : (k + 1) * TILE]

            if i > 0:
                send_pair(block_of(i - 1))
        y_recv[part][my_y] = y_send[part][my_y]
        send_pair(block_of(blocks - 1))

    def y_any(part, g):
        return pltpu.make_async_remote_copy(
            y_send[part].at[0], y_recv[part].at[g], y_send_sem.at[part], y_recv_sem.at[part, g],
            device_id={"head": 0}, device_id_type=MESH,
        )

    for n in range(count - WINDOW, count):
        windowed(n).wait_send()

    @pl.loop(0, 2 * (SEQ - 1) - count)
    def _(r):
        v_copy(0, 0, v_send_sem.at[0]).wait_send()

    for part in range(1, PARTS):

        @pl.loop(0, SEQ - 1)
        def _(r):
            v_copy(part, 0, v_send_sem.at[part]).wait_send()

    @pl.when(me == 0)
    def _():
        for p in range(1, PLANE):
            from_root(p).wait_send()

    @pl.when(up)
    def _():
        along(1, 0).wait_send()

    @pl.when(down)
    def _():
        along(ZS - 1, 1).wait_send()

    @pl.loop(0, PLANE)
    def _(q):
        @pl.when(jnp.logical_and(q != piece, z * PLANE + q != 0))
        def _():
            in_plane(q).wait_send()

    for part in range(PARTS):

        @pl.loop(0, YS)
        def _(g):
            @pl.when(g != my_y)
            def _():
                y_any(part, g).wait_recv()

        @pl.loop(0, YS - 1)
        def _(r):
            y_any(part, 0).wait_send()


def identity():
    rows = lax.broadcasted_iota(jnp.int32, (TILE, TILE), 0)
    return (rows == lax.broadcasted_iota(jnp.int32, (TILE, TILE), 1)).astype(jnp.bfloat16)


def flip(matrix):
    return lax.dot_general(
        identity(), matrix, (((1,), (1,)), ((), ())), preferred_element_type=jnp.float32
    ).astype(jnp.bfloat16)


def arrange(*refs):
    out_ref = refs[-1]
    for g in range(YS):
        for h in range(HEADS):
            rows = [
                ref[g, h * d_size : (h + 1) * d_size] for ref, (_, d_size) in zip(refs, SPLITS)
            ]
            lo = (g * HEADS + h) * HD
            out_ref[:, lo : lo + HD] = flip(jnp.concatenate(rows, 0))


def body(queries, keys, values, tile_pool, tile_lists, key_slot):
    anywhere = pl.BlockSpec(memory_space=pl.ANY)
    vmem = pl.BlockSpec(memory_space=pltpu.VMEM)
    bf16, f32, i32 = jnp.bfloat16, jnp.float32, jnp.int32
    dma = pltpu.SemaphoreType.DMA
    sizes = [d_size for _, d_size in SPLITS]
    v_bufs = [pltpu.VMEM((SEQ, d, TILE), bf16) for d in sizes]
    y_bufs = [pltpu.VMEM((TILES, HEADS * d, TILE), bf16) for d in sizes]
    key_slot = key_slot.reshape(1, -1)
    received = pl.pallas_call(
        kernel,
        out_shape=[jax.ShapeDtypeStruct((YS, HEADS * d, TILE), bf16) for d in sizes],
        in_specs=[anywhere] * 6,
        out_specs=[vmem] * PARTS,
        scratch_shapes=v_bufs
        + v_bufs
        + y_bufs
        + [
            pltpu.VMEM(queries.shape, bf16),
            pltpu.VMEM(keys.shape, bf16),
            pltpu.VMEM(values.shape, bf16),
            pltpu.VMEM(tile_pool.shape, i32),
            pltpu.VMEM(tile_lists.shape, i32),
            pltpu.VMEM(key_slot.shape, i32),
            pltpu.SMEM(tile_pool.shape, i32),
            pltpu.SMEM(key_slot.shape, i32),
            pltpu.VMEM((1, SEQ * POOL), i32),
            pltpu.SMEM((1, SEQ * POOL), i32),
            pltpu.VMEM((SEQ, TILE, HD), bf16),
            pltpu.VMEM((SEQ, TILE, HD), bf16),
            pltpu.VMEM((PLANE, HEADS * TILE, TILE), bf16),
            pltpu.VMEM((HEADS * TILES, TILE, HD), bf16),
            pltpu.VMEM((HEADS * TILES, HD, TILE), bf16),
            pltpu.VMEM((HEADS, POOL, TILES * TILE), f32),
            pltpu.VMEM((KEYS * TILE, HD), bf16),
            pltpu.VMEM((HEADS, max(sizes), KEYS * TILE), bf16),
            pltpu.VMEM((HEADS, KEYS * TILE, TILES * TILE), bf16),
            pltpu.VMEM((KEYS * TILE, QB), f32),
            pltpu.VMEM((HEADS, 1, TILES * TILE), f32),
            dma((8,)),
            dma,
            dma((WINDOW,)),
            dma((SEQ,)),
            dma((PARTS,)),
            dma((PARTS, SEQ)),
            dma((2,)),
            dma,
            dma((2 * PLANE,)),
            dma((PLANE,)),
            dma((PARTS,)),
            dma((PARTS, YS)),
        ],
        compiler_params=pltpu.CompilerParams(
            collective_id=0, has_side_effects=True, vmem_limit_bytes=56 * 2**20
        ),
        name="attend",
    )(queries, keys, values, tile_pool, tile_lists, key_slot)
    return pl.pallas_call(
        arrange,
        out_shape=jax.ShapeDtypeStruct((TILE, YS * HEADS * HD), bf16),
        in_specs=[vmem] * PARTS,
        out_specs=vmem,
        name="arrange",
    )(*received)


def solution(mesh):
    return jax.shard_map(
        body,
        mesh=mesh,
        in_specs=(
            P("seq", "head"),
            P("seq", "head"),
            P("seq", "head"),
            P("head", None),
            P("head", "seq", None),
            P(),
        ),
        out_specs=P(("seq", "head"), None),
        check_vma=False,
    )
```
